32 devices in a mesh: dp: 4 (over x, core), fsdp: 8 (over z, y).
Axes of the slice: x: 2, y: 2, z: 4, core: 2. Of those that a mesh axis runs over, the one named last changes fastest.
Arguments:
- inputs: bfloat16 [2, 32, 512, 768], P(None, ('dp', 'fsdp')), may hold values from -6 to 6
- segments: int32 [2, 32, 512], P(None, ('dp', 'fsdp')), may hold values from 0 to 5, never falling along the last dimension, each value on 1 to 256 neighbouring positions
- query_weight: bfloat16 [768, 768], P(('dp', 'fsdp')), may hold values from -0.3125 to 0.3125
- query_bias: bfloat16 [768], P(('dp', 'fsdp')), may hold values from -3 to 3
- key_weight: bfloat16 [768, 768], P(('dp', 'fsdp')), may hold values from -0.3125 to 0.3125
- value_weight: bfloat16 [768, 768], P(('dp', 'fsdp')), may hold values from -0.21875 to 0.21875
- value_bias: bfloat16 [768], P(('dp', 'fsdp')), may hold values from -3 to 3
- output_weight: bfloat16 [768, 768], P(('dp', 'fsdp')), may hold values from -0.875 to 0.875
- output_bias: bfloat16 [768], P(('dp', 'fsdp')), may hold values from -3 to 3
- norm_gain: bfloat16 [768], P(('dp', 'fsdp')), may hold values from 0.099609375 to 1.8984375
- norm_shift: bfloat16 [768], P(('dp', 'fsdp')), may hold values from -3 to 3
- inner_weight: bfloat16 [768, 3072], P(('dp', 'fsdp')), may hold values from -0.21875 to 0.21875
- inner_bias: bfloat16 [3072], P(('dp', 'fsdp')), may hold values from -3 to 3
- outer_weight: bfloat16 [3072, 768], P(('dp', 'fsdp')), may hold values from -0.109375 to 0.109375
- outer_bias: bfloat16 [768], P(('dp', 'fsdp')), may hold values from -3 to 3
- final_gain: bfloat16 [768], P(('dp', 'fsdp')), may hold values from 0.099609375 to 1.8984375
- final_shift: bfloat16 [768], P(('dp', 'fsdp')), may hold values from -3 to 3
- cotangent: bfloat16 [2, 32, 512, 768], P(None, ('dp', 'fsdp')), may hold values from -6 to 6
Outputs:
- layer_output: bfloat16 [2, 32, 512, 768], P(None, ('dp', 'fsdp'))
- input_grad: bfloat16 [2, 32, 512, 768], P(None, ('dp', 'fsdp'))
- query_weight_grad: float32 [768, 768], P(('dp', 'fsdp'))
- query_bias_grad: float32 [768], P(('dp', 'fsdp'))
- key_weight_grad: float32 [768, 768], P(('dp', 'fsdp'))
- value_weight_grad: float32 [768, 768], P(('dp', 'fsdp'))
- value_bias_grad: float32 [768], P(('dp', 'fsdp'))
- output_weight_grad: float32 [768, 768], P(('dp', 'fsdp'))
- output_bias_grad: float32 [768], P(('dp', 'fsdp'))
- norm_gain_grad: float32 [768], P(('dp', 'fsdp'))
- norm_shift_grad: float32 [768], P(('dp', 'fsdp'))
- inner_weight_grad: float32 [768, 3072], P(('dp', 'fsdp'))
- inner_bias_grad: float32 [3072], P(('dp', 'fsdp'))
- outer_weight_grad: float32 [3072, 768], P(('dp', 'fsdp'))
- outer_bias_grad: float32 [768], P(('dp', 'fsdp'))
- final_gain_grad: float32 [768], P(('dp', 'fsdp'))
- final_shift_grad: float32 [768], P(('dp', 'fsdp'))
The draws below stay inside these ranges and needn't reach their ends.
Inputs may be any that keep to these rules, and one draw needn't show every extreme that they name: `segments`: in each packed row segment numbers never fall, every one of the 6 numbers is used, and each segment has 1 to 256 positions, one exactly 256.
All inputs are finite; a program needn't handle non-finite values.
Results may differ from the reference program's by a relative error of at most 0.014.
The reference program's roundings to bfloat16 on the way count: a program that leaves them out, or rounds other values in their place, can miss the bound.
Values may be sent and summed in bfloat16 or wider, within the bound.
No kernel may reach another device: no remote copies, remote signals or barrier semaphores. Data moves between devices by JAX's collectives and lax.ppermute only.
A program may use at most 192 MiB of HBM per device.

```python
import math
import jax
import jax.numpy as jnp
import numpy as np
from jax import lax

D = 768
HEADS = 12
HEAD_DIM = 64
FF = 3072
SEQ = 512
MB = 2
DOCS = 6
LONGEST = 256
ROWS = 32


def raised(result, key, source, target, blocks, factor):
    def block_of(dim):
        return (jnp.arange(result.shape[dim]) // (result.shape[dim] // blocks)).reshape((-1,) + (1,) * (result.ndim - 1 - dim))

    one_side = jax.random.permutation(key, blocks)[block_of(target)]
    other_side = (block_of(target) + blocks // 2) % blocks
    return jnp.where((block_of(source) == one_side) | (block_of(source) == other_side), factor * result, result)


def levels(rng, shape, split, low, high):
    def one(position, blocks):
        draws = jax.random.uniform(jax.random.fold_in(jax.random.fold_in(rng, 6), position), (blocks,), jnp.float32, low / len(split), high / len(split))
        return jnp.repeat(jnp.exp(draws), shape[position] // blocks).reshape((-1,) + (1,) * (len(shape) - position - 1))

    loudness = one(*split[0])
    for cut in split[1:]:
        loudness = loudness * one(*cut)
    return loudness


def split_up(number_of, total, reach, lean):
    loads = [(1 << 20) // math.isqrt(grade ** lean) + 1 for grade in range(2, number_of + 1)]
    surplus, counts = total - reach - (number_of - 1), [1] * (number_of - 1)
    while surplus > 0:
        free = [i for i in range(number_of - 1) if counts[i] < reach]
        pool, budget = sum([loads[i] for i in free]), surplus
        for i in free:
            extra = min(reach - counts[i], max(1, budget * loads[i] // pool), surplus)
            counts[i] = counts[i] + extra
            surplus = surplus - extra
    return np.array([reach] + counts)


def ragged_sizes(key, count, total, limit, slope):
    if count == 2:
        one = jax.random.randint(key, (), max(1, total - limit), min(limit, total - 1) + 1)
        return jnp.stack([one, total - one])
    tallies = jnp.asarray(split_up(count, total, limit, slope), jnp.int32)
    couples = (count - 1) // 2
    source_of, receiver = tallies[1:1 + 2 * couples:2], tallies[2:2 + 2 * couples:2]
    room = jnp.minimum(source_of - 1, limit - receiver)
    moved = jax.random.randint(jax.random.fold_in(key, 1), (couples,), 0, 1 << 20) % (room + 1)
    tallies = tallies.at[1:1 + 2 * couples:2].set(source_of - moved).at[2:2 + 2 * couples:2].set(receiver + moved)
    return tallies[jax.random.permutation(jax.random.fold_in(key, 2), count)]


def bell_draw(key, extent, scale, limit, shards=(), kind=jnp.bfloat16):
    values = scale * jax.random.normal(key, extent, jnp.float32)
    if shards:
        values = values * levels(key, extent, shards, -0.22, 0.18)
    return jnp.clip(values, -limit, limit).astype(kind)


def bell_draw_with(own_key, shape, width, most, pieces, heavy, held_as=jnp.bfloat16):
    result = width * jax.random.normal(own_key, shape, jnp.float32)
    if pieces:
        result = result * levels(own_key, shape, pieces, -0.22, 0.18)
    return jnp.clip(raised(result, jax.random.fold_in(own_key, 3), *heavy), -most, most).astype(held_as)


def setup_inputs(seed: int = 0) -> dict:
    splits = jax.random.split(jax.random.key(seed), 19)
    inputs = bell_draw_with(splits[0], (MB, ROWS, SEQ, D), 1.0, 6.0, ((1, 32),), (1, 3, 32, 2.75))
    segments = jax.vmap(lambda own: jnp.searchsorted(jnp.cumsum(ragged_sizes(own, DOCS, SEQ, LONGEST, 2)), jnp.arange(SEQ), side="right"))(jax.random.split(splits[1], MB * ROWS)).reshape((MB, ROWS, SEQ)).astype(jnp.int32)
    query_weight = bell_draw(splits[2], (D, D), (D // 2) ** -0.5, 0.3125, ((0, 32),))
    query_bias = bell_draw(splits[3], (D,), 0.5, 3.0, ((0, 32),))
    key_weight = bell_draw(splits[4], (D, D), (D // 2) ** -0.5, 0.3125, ((0, 32),))
    value_weight = bell_draw(splits[5], (D, D), D ** -0.5, 0.21875, ((0, 32),))
    value_bias = bell_draw(splits[6], (D,), 0.5, 3.0, ((0, 32),))
    output_weight = bell_draw(splits[7], (D, D), (D // 16) ** -0.5, 0.875, ((0, 32),))
    output_bias = bell_draw(splits[8], (D,), 0.5, 3.0, ((0, 32),))
    norm_gain = jnp.clip(1.0 + 0.18 * jax.random.normal(splits[9], (D,), jnp.float32), 0.099609375, 1.8984375).astype(jnp.bfloat16)
    norm_shift = bell_draw(splits[10], (D,), 0.5, 3.0, ((0, 32),))
    inner_weight = bell_draw(splits[11], (D, FF), D ** -0.5, 0.21875, ((0, 32),))
    inner_bias = bell_draw(splits[12], (FF,), 0.5, 3.0, ((0, 32),))
    outer_weight = bell_draw(splits[13], (FF, D), FF ** -0.5, 0.109375, ((0, 32),))
    outer_bias = bell_draw(splits[14], (D,), 0.5, 3.0, ((0, 32),))
    final_gain = jnp.clip(1.0 + 0.18 * jax.random.normal(splits[15], (D,), jnp.float32), 0.099609375, 1.8984375).astype(jnp.bfloat16)
    final_shift = bell_draw(splits[16], (D,), 0.5, 3.0, ((0, 32),))
    cotangent = bell_draw_with(splits[17], (MB, ROWS, SEQ, D), 1.0, 6.0, ((1, 32),), (1, 3, 32, 2.75))
    return dict(inputs=inputs, segments=segments, query_weight=query_weight, query_bias=query_bias, key_weight=key_weight, value_weight=value_weight, value_bias=value_bias, output_weight=output_weight, output_bias=output_bias, norm_gain=norm_gain, norm_shift=norm_shift, inner_weight=inner_weight, inner_bias=inner_bias, outer_weight=outer_weight, outer_bias=outer_bias, final_gain=final_gain, final_shift=final_shift, cotangent=cotangent)


@jax.custom_vjp
def low(v):
    return lax.optimization_barrier(v.astype(jnp.bfloat16)).astype(jnp.float32)

@jax.custom_vjp
def low_back(v):
    return v

def low_keep(v):
    return (low(v), None)

def low_pass(kept, grad):
    return (grad,)

def back_keep(v):
    return (v, None)

def back_low(kept, grad):
    return (low(grad),)
low.defvjp(low_keep, low_pass)
low_back.defvjp(back_keep, back_low)

def project(left, right):
    return jnp.einsum('rsd,de->rse', left, right, precision=lax.Precision.HIGHEST)

def normalize(hidden, scale_vec, shift_vec):
    centre = lax.optimization_barrier(jnp.mean(hidden, axis=-1, keepdims=True))
    shifted = hidden - centre
    spread = lax.optimization_barrier(jnp.mean(shifted * shifted, axis=-1, keepdims=True))
    return shifted * lax.rsqrt(spread + 1e-05) * scale_vec + shift_vec

def encoder(weight_set, layer_inputs, segment_ids):
    query_weight, query_bias, key_weight, value_weight, value_bias, output_weight, output_bias, norm_gain, norm_shift, inner_weight, inner_bias, outer_weight, outer_bias, final_gain, final_shift = weight_set
    row_count, row_length, model_width = layer_inputs.shape

    def split_heads(tensor):
        return tensor.reshape(row_count, row_length, HEADS, HEAD_DIM)
    queries = low(low_back(project(layer_inputs, query_weight) + query_bias))
    keys_all = low(low_back(project(layer_inputs, key_weight)))
    values_all = low(low_back(project(layer_inputs, value_weight) + value_bias))
    scores = jnp.einsum('rqhd,rkhd->rhqk', split_heads(queries), split_heads(keys_all), precision=lax.Precision.HIGHEST)
    scores = low_back(scores * HEAD_DIM ** (-0.5))
    same_segment = segment_ids[:, None, :, None] == segment_ids[:, None, None, :]
    scores = jnp.where(same_segment, scores, -1000000000.0)
    row_peak = lax.optimization_barrier(jnp.max(scores, axis=-1, keepdims=True))
    exponent = jnp.exp(scores - row_peak)
    attention = exponent / lax.optimization_barrier(jnp.sum(exponent, axis=-1, keepdims=True))
    context = jnp.einsum('rhqk,rkhd->rqhd', low(attention), split_heads(values_all), precision=lax.Precision.HIGHEST)
    context = low(low_back(context.reshape(row_count, row_length, model_width)))
    attended = low_back(project(context, output_weight) + output_bias)
    normed_one = normalize(layer_inputs + attended, norm_gain, norm_shift)
    hidden_in = low_back(project(low(normed_one), inner_weight) + inner_bias)
    activated = low(jax.nn.gelu(hidden_in, approximate=True))
    outer_out = low_back(project(activated, outer_weight) + outer_bias)
    return normalize(normed_one + outer_out, final_gain, final_shift)

def reference(inputs, segments, query_weight, query_bias, key_weight, value_weight, value_bias, output_weight, output_bias, norm_gain, norm_shift, inner_weight, inner_bias, outer_weight, outer_bias, final_gain, final_shift, cotangent):
    weights = tuple((weight_array.astype(jnp.float32) for weight_array in (query_weight, query_bias, key_weight, value_weight, value_bias, output_weight, output_bias, norm_gain, norm_shift, inner_weight, inner_bias, outer_weight, outer_bias, final_gain, final_shift)))
    group_rows = 8
    flat_inputs = inputs.astype(jnp.float32).reshape(-1, group_rows, SEQ, D)
    flat_segments = segments.reshape(-1, group_rows, SEQ)
    blockwise = jax.checkpoint(encoder)

    def whole(weight_set, layer_inputs):

        def apply_member(member):
            return blockwise(weight_set, member[0], member[1])
        return lax.map(apply_member, (layer_inputs, flat_segments))
    outputs, pullback = jax.vjp(whole, weights, flat_inputs)
    weight_grads, grad_inputs = pullback(cotangent.astype(jnp.float32).reshape(flat_inputs.shape))
    return (outputs.reshape(inputs.shape).astype(jnp.bfloat16), grad_inputs.reshape(inputs.shape).astype(jnp.bfloat16), weight_grads[0], weight_grads[1], weight_grads[2], weight_grads[3], weight_grads[4], weight_grads[5], weight_grads[6], weight_grads[7], weight_grads[8], weight_grads[9], weight_grads[10], weight_grads[11], weight_grads[12], weight_grads[13], weight_grads[14])
```

```python
import functools

import jax
import jax.numpy as jnp
from jax import lax
from jax.experimental import pallas as pl
from jax.experimental.pallas import tpu as pltpu
from jax.sharding import PartitionSpec as P

AXES = ("dp", "fsdp")
F32 = jnp.float32
BF = jnp.bfloat16


def dot(a, b, ca, cb):
    return lax.dot_general(a, b, (((ca,), (cb,)), ((), ())), preferred_element_type=F32)


def attn_fwd_kernel(segr_ref, segc_ref, q_ref,k_ref,v_ref,o_ref,l_ref,bias_ref, *, TQ):
    S=q_ref.shape[0]
    @pl.when(pl.program_id(1)==0)
    def _():
        bias_ref[...]=jnp.where(segc_ref[...]==segr_ref[...],0.0,-1e9)
    lane=lax.broadcasted_iota(jnp.int32,(S,128),1)
    q=q_ref[...]*jnp.asarray(0.125,BF); k=k_ref[...]; v=v_ref[...]
    z=jnp.zeros_like(k)
    for t in range(S//TQ):
        sl=slice(t*TQ,(t+1)*TQ)
        ctx=[]
        for h in range(2):
            m=(lane<64) if h==0 else (lane>=64)
            kh=jnp.where(m,k,z); vh=jnp.where(m,v,z)
            s=dot(kh,q[sl],1,1)+bias_ref[:,sl]
            mx=jnp.max(s,axis=0,keepdims=True)
            e=jnp.exp(s-mx)
            tot=jnp.sum(e,axis=0,keepdims=True)
            p=(e*(1.0/tot)).astype(BF)
            l_ref[h:h+1,sl]=mx+jnp.log(tot)
            ctx.append(dot(vh,p,0,0))
        o_ref[sl,:]=(ctx[0]+ctx[1]).T.astype(BF)

def attn_fwd(q,k,v,segr,segc,TQ=512):
    T,D=q.shape; S=segr.shape[-1]; R=T//S; HP=D//128
    blk=pl.BlockSpec((S,128),lambda r,h:(r,h))
    return pl.pallas_call(functools.partial(attn_fwd_kernel,TQ=TQ),
        grid=(R,HP),
        in_specs=[pl.BlockSpec((None,1,S),lambda r,h:(r,0,0)),pl.BlockSpec((None,S,1),lambda r,h:(r,0,0)),blk,blk,blk],
        out_specs=[blk,pl.BlockSpec((None,None,2,S),lambda r,h:(r,h,0,0))],
        out_shape=[jax.ShapeDtypeStruct((T,D),BF),jax.ShapeDtypeStruct((R,HP,2,S),F32)],
        scratch_shapes=[pltpu.VMEM((S,S),F32)],
        name="attn_fwd")(segr,segc,q,k,v)

def attn_bwd_kernel(segr_ref, segc_ref, q_ref,k_ref,v_ref,g_ref,l_ref,dq_ref,dk_ref,dv_ref,bias_ref, *, TQ):
    S=q_ref.shape[0]
    @pl.when(pl.program_id(1)==0)
    def _():
        bias_ref[...]=jnp.where(segc_ref[...]==segr_ref[...],0.0,-1e9)
    lane=lax.broadcasted_iota(jnp.int32,(S,128),1)
    q=q_ref[...]*jnp.asarray(0.125,BF); k=k_ref[...]; v=v_ref[...]; g=g_ref[...]
    z=jnp.zeros_like(k)
    dk=None; dv=None
    for t in range(S//TQ):
        sl=slice(t*TQ,(t+1)*TQ)
        dqs=[]
        for h in range(2):
            m=(lane<64) if h==0 else (lane>=64)
            kh=jnp.where(m,k,z); vh=jnp.where(m,v,z)
            qh=jnp.where(m[sl],q[sl],z[sl]); gh=jnp.where(m[sl],g[sl],z[sl])
            s=dot(kh,q[sl],1,1)+bias_ref[:,sl]
            p=jnp.exp(s-l_ref[h:h+1,sl])
            dp=dot(vh,g[sl],1,1)
            pb=p.astype(BF)
            dsum=jnp.sum(p*dp,axis=0,keepdims=True)
            ds=(p*(dp-dsum)).astype(BF)
            dvc=dot(pb,gh,1,0)
            dkc=dot(ds,qh,1,0)
            dqs.append(dot(kh,ds,0,0))
            dk=dkc if dk is None else dk+dkc
            dv=dvc if dv is None else dv+dvc
        dq_ref[sl,:]=((dqs[0]+dqs[1])*0.125).T.astype(BF)
    dk_ref[...]=dk.astype(BF); dv_ref[...]=dv.astype(BF)

def attn_bwd(q,k,v,g,l,segr,segc,TQ=512):
    T,D=q.shape; S=segr.shape[-1]; R=T//S; HP=D//128
    blk=pl.BlockSpec((S,128),lambda r,h:(r,h))
    return pl.pallas_call(functools.partial(attn_bwd_kernel,TQ=TQ),
        grid=(R,HP),
        in_specs=[pl.BlockSpec((None,1,S),lambda r,h:(r,0,0)),pl.BlockSpec((None,S,1),lambda r,h:(r,0,0)),blk,blk,blk,blk,pl.BlockSpec((None,None,2,S),lambda r,h:(r,h,0,0))],
        out_specs=[blk]*3,
        out_shape=[jax.ShapeDtypeStruct((T,D),BF)]*3,
        scratch_shapes=[pltpu.VMEM((S,S),F32)],
        name="attn_bwd")(segr,segc,q,k,v,g,l)


def normal_parts(hidden):
    centre = jnp.mean(hidden, axis=-1, keepdims=True)
    shifted = hidden - centre
    spread = jnp.mean(shifted * shifted, axis=-1, keepdims=True)
    inv = lax.rsqrt(spread + 1e-05)
    return shifted * inv, inv


def normal_back(grad, gain, z, inv):
    e = grad * gain
    return inv * (e - jnp.mean(e, -1, keepdims=True) - z * jnp.mean(e * z, -1, keepdims=True))


def gelu_both(u):
    c = 0.7978845608028654
    inner = c * (u + 0.044715 * u * u * u)
    t = jnp.tanh(inner)
    act = 0.5 * u * (1.0 + t)
    slope = 0.5 * (1.0 + t) + 0.5 * u * (1.0 - t * t) * c * (1.0 + 3 * 0.044715 * u * u)
    return act, slope


def body(inputs, segments, wq, bq, wk, wv, bv, wo, bo, g1, c1, wi, bi, wu, bu, g2, c2, cotangent):
    micro, rows, seq, width = inputs.shape
    shard = wq.shape[0]
    ff = wi.shape[1]
    wide = ff // width
    vectors = (bq, bv, bo, g1, c1, bi, bu, g2, c2)
    small = jnp.concatenate([v.reshape(shard, -1) for v in vectors], axis=1)
    small_cols = small.shape[1]
    small = jnp.pad(small, ((0, 0), (0, 128 - small_cols)))
    packed = jnp.concatenate([wq, wk, wv, wo, wi, wu.reshape(shard, -1), small], axis=1)
    full = lax.all_gather(packed, AXES, axis=0, tiled=True)
    Wqkv = full[:, : 3 * width]
    Wo = full[:, 3 * width : 4 * width]
    Wi = full[:, 4 * width : 4 * width + ff]
    Wu = full[:, 4 * width + ff : 4 * width + 2 * ff].reshape(ff, width)
    sm = full[:, 4 * width + 2 * ff :]
    vecs = []
    at = 0
    for v in vectors:
        n = v.shape[0] // shard
        vecs.append(sm[:, at : at + n].reshape(-1).astype(F32))
        at += n
    Bq, Bv, Bo, G1, C1, Bi, Bu, G2, C2 = vecs

    x = inputs.reshape(-1, width)
    cot = cotangent.reshape(-1, width).astype(F32)
    seg = segments.reshape(micro * rows, seq)
    segr, segc = seg[:, None, :], seg[:, :, None]

    Bqkv = jnp.concatenate([Bq, jnp.zeros_like(Bq), Bv])
    qkv = (dot(x, Wqkv, 1, 0) + Bqkv).astype(BF)
    q, k, v = qkv[:, :width], qkv[:, width : 2 * width], qkv[:, 2 * width :]
    ctx, lse = attn_fwd(q, k, v, segr, segc)
    resid1 = x.astype(F32) + dot(ctx, Wo, 1, 0) + Bo
    z1, inv1 = normal_parts(resid1)
    norm1 = z1 * G1 + C1
    low1 = norm1.astype(BF)
    hidden = dot(low1, Wi, 1, 0) + Bi
    act, slope = gelu_both(hidden)
    act = act.astype(BF)
    resid2 = norm1 + dot(act, Wu, 1, 0) + Bu
    z2, inv2 = normal_parts(resid2)
    out = (z2 * G2 + C2).astype(BF)

    dg2 = jnp.sum(cot * z2, 0)
    dc2 = jnp.sum(cot, 0)
    grad2 = normal_back(cot, G2, z2, inv2)
    low2 = grad2.astype(BF)
    dbu = jnp.sum(low2.astype(F32), 0)
    dWu = dot(act, low2, 0, 0)
    ilow = (dot(low2, Wu, 1, 1) * slope).astype(BF)
    dbi = jnp.sum(ilow.astype(F32), 0)
    dWi = dot(low1, ilow, 0, 0)
    gfirst = grad2 + dot(ilow, Wi, 1, 1)
    dg1 = jnp.sum(gfirst * z1, 0)
    dc1 = jnp.sum(gfirst, 0)
    grad1 = normal_back(gfirst, G1, z1, inv1)
    alow = grad1.astype(BF)
    dbo = jnp.sum(alow.astype(F32), 0)
    dWo = dot(ctx, alow, 0, 0)
    gctx = dot(alow, Wo, 1, 1).astype(BF)
    dq, dk, dv = attn_bwd(q, k, v, gctx, lse, segr, segc)
    dbq = jnp.sum(dq.astype(F32), 0)
    dbv = jnp.sum(dv.astype(F32), 0)
    dWq, dWk, dWv = (dot(x, t, 0, 0) for t in (dq, dk, dv))
    dx = (
        grad1
        + dot(dq, Wqkv[:, :width], 1, 1)
        + dot(dk, Wqkv[:, width : 2 * width], 1, 1)
        + dot(dv, Wqkv[:, 2 * width :], 1, 1)
    ).astype(BF)

    gsmall = jnp.concatenate(
        [t.reshape(width, -1) for t in (dbq, dbv, dbo, dg1, dc1, dbi, dbu, dg2, dc2)], axis=1
    )
    gsmall = jnp.pad(gsmall, ((0, 0), (0, 128 - small_cols)))
    gpack = jnp.concatenate(
        [t.astype(BF) for t in (dWq, dWk, dWv, dWo, dWi, dWu.reshape(width, -1), gsmall)], axis=1
    )
    mine = lax.psum_scatter(gpack, AXES, scatter_dimension=0, tiled=True).astype(F32)
    gs = mine[:, 4 * width + 2 * ff :]
    gv = []
    at = 0
    for v in vectors:
        n = v.shape[0] // shard
        gv.append(gs[:, at : at + n].reshape(-1))
        at += n
    return (
        out.reshape(inputs.shape), dx.reshape(inputs.shape),
        mine[:, :width], gv[0], mine[:, width : 2 * width], mine[:, 2 * width : 3 * width], gv[1],
        mine[:, 3 * width : 4 * width], gv[2], gv[3], gv[4],
        mine[:, 4 * width : 4 * width + ff], gv[5],
        mine[:, 4 * width + ff : 4 * width + 2 * ff].reshape(wu.shape), gv[6], gv[7], gv[8],
    )


MAT = P(AXES, None)
VEC = P(AXES)
ACT = P(None, AXES, None, None)


def solution(mesh):
    weights = (MAT, VEC, MAT, MAT, VEC, MAT, VEC, VEC, VEC, MAT, VEC, MAT, VEC, VEC, VEC)
    return jax.shard_map(
        body,
        mesh=mesh,
        in_specs=(ACT, P(None, AXES, None)) + weights + (ACT,),
        out_specs=(ACT, ACT) + weights,
        check_vma=False,
    )
```
